32 devices in a mesh: dp: 8 (over z, x), grp: 4 (over y, core).
Axes of the slice: x: 2, y: 2, z: 4, core: 2. Of those that a mesh axis runs over, the one named last changes fastest.
Arguments:
- x_in: bfloat16 [4096, 1600], P('dp'), may hold values from -6 to 6
- attn_in: bfloat16 [4096, 1600], P('dp', 'grp'), may hold values from -6 to 6
- grad_qkv: bfloat16 [4096, 4800], P('dp', 'grp'), may hold values from -80 to 80
- grad_out: bfloat16 [4096, 1600], P('dp'), may hold values from -80 to 80
- owner: int32 [64], replicated, may hold values from 0 to 7, as said below
- step: int32 [1], replicated, may hold values from 1 to 29
- master: float32 [4, 128, 200, 200], P('grp', 'dp'), may hold values from -0.125 to 0.125
- moment: float32 [4, 128, 200, 200], P('grp', 'dp'), may hold values from -0.3125 to 0.3125
- second: float32 [4, 128, 200, 200], P('grp', 'dp'), may hold values from 0.003 to 0.1
- stat_left: float32 [4, 128, 200, 200], P('grp', 'dp'), may hold values from -8 to 32, as said below
- stat_right: float32 [4, 128, 200, 200], P('grp', 'dp'), may hold values from -8 to 32, as said below
- root_left: float32 [4, 128, 200, 200], P('grp', 'dp'), may hold values from -1 to 4, as said below
- root_right: float32 [4, 128, 200, 200], P('grp', 'dp'), may hold values from -1 to 4, as said below
- qkv_bias: float32 [4800], P('grp'), may hold values from -3 to 3
- qkv_bias_m: float32 [4800], P('grp'), may hold values from -1.25 to 1.25
- qkv_bias_v: float32 [4800], P('grp'), may hold values from 0.01 to 0.3
- proj_bias: float32 [1600], replicated, may hold values from -3 to 3
- proj_bias_m: float32 [1600], replicated, may hold values from -1.25 to 1.25
- proj_bias_v: float32 [1600], replicated, may hold values from 0.01 to 0.3
Outputs:
- master_new: float32 [4, 128, 200, 200], P('grp', 'dp')
- moment_new: float32 [4, 128, 200, 200], P('grp', 'dp')
- second_new: float32 [4, 128, 200, 200], P('grp', 'dp')
- stat_left_new: float32 [4, 128, 200, 200], P('grp', 'dp')
- stat_right_new: float32 [4, 128, 200, 200], P('grp', 'dp')
- qkv_weight: bfloat16 [1600, 4800], P(None, 'grp')
- proj_weight: bfloat16 [1600, 1600], P('grp')
- qkv_bias_new: float32 [4800], P('grp')
- qkv_bias_m_new: float32 [4800], P('grp')
- qkv_bias_v_new: float32 [4800], P('grp')
- proj_bias_new: float32 [1600], replicated
- proj_bias_m_new: float32 [1600], replicated
- proj_bias_v_new: float32 [1600], replicated
The draws below stay inside these ranges and needn't reach their ends.
Inputs may be any that keep to these rules, and one draw needn't show every extreme that they name: `owner`: every index of dp owns at most 16 blocks, and one owns exactly 16. `stat_left`: symmetric. `stat_right`: symmetric. `root_left`: symmetric. `root_right`: symmetric.
All inputs are finite; a program needn't handle non-finite values.
Results may differ from the reference program's by a relative error of at most 0.0004.
Values may be sent and summed in bfloat16 or wider, within the bound.
A program may use at most 192 MiB of HBM per device.

```python
import math
import jax
import jax.numpy as jnp
from jax import lax

D = 1600
BLK = 200
TOKENS = 4096
NQ = 48
NBLK = 64
SLOTS = 16
N_DP = 8
N_GRP = 4


def draw_owner(key, part):
    spots = N_DP * SLOTS
    key_full, key_order, key_blocks = jax.random.split(jax.random.fold_in(key, 17), 3)
    full_device = jax.random.randint(key_full, (), 0, N_DP)
    device_of = jnp.arange(spots, dtype=jnp.int32) // SLOTS
    shuffled = jax.random.permutation(key_order, spots).astype(jnp.int32)
    scores = jnp.where(device_of == full_device, jnp.arange(spots, dtype=jnp.int32) - spots, shuffled)
    order = jnp.argsort(scores, stable=True)
    chosen = (order[:NBLK] // SLOTS).astype(jnp.int32)
    block_order = jax.random.permutation(key_blocks, NBLK)
    return jnp.zeros((NBLK,), jnp.int32).at[block_order].set(chosen)


def symmetric_blocks(key, low, high, level):
    shape = (N_GRP, N_DP * SLOTS, BLK, BLK)
    key_diag, key_off = jax.random.split(key)
    diag = jnp.exp(jax.random.uniform(key_diag, shape[:3], jnp.float32, jnp.log(low), jnp.log(high)))
    off = jnp.clip(jax.random.normal(key_off, shape, jnp.float32), -4.0, 4.0)
    off = (off + jnp.swapaxes(off, 2, 3)) * (0.3 / (2.0 * BLK) ** 0.5)
    unit = jnp.eye(BLK, dtype=jnp.float32)
    return level * (unit * diag[..., None] + (1.0 - unit) * off)


def draw_stat_left(key, part):
    return symmetric_blocks(jax.random.fold_in(key, 21), 0.5, 2.0, 0.04 * BLK)


def draw_stat_right(key, part):
    return symmetric_blocks(jax.random.fold_in(key, 22), 0.5, 2.0, 0.04 * BLK)


def draw_root_left(key, part):
    return symmetric_blocks(jax.random.fold_in(key, 23), 1.0, 2.0, 1.0)


def draw_root_right(key, part):
    return symmetric_blocks(jax.random.fold_in(key, 24), 1.0, 2.0, 1.0)


def shard_levels(own_key, dims, shards, smallest, largest):
    factor_of, own = 1.0, jax.random.fold_in(own_key, 6)
    for dim, parts in shards:
        heights = jnp.exp(jax.random.uniform(jax.random.fold_in(own, dim), (parts,), jnp.float32, smallest / len(shards), largest / len(shards)))
        factor_of = factor_of * jnp.repeat(heights, dims[dim] // parts).reshape([-1 if axis == dim else 1 for axis in range(len(dims))])
    return factor_of


def bell_draw(key, dims, deviation, most, pieces=(), kind=jnp.bfloat16):
    gain = shard_levels(key, dims, pieces, -0.22, 0.18) if pieces else 1.0
    drawn = jax.random.normal(key, dims, jnp.float32) * deviation * gain
    return jnp.minimum(jnp.maximum(drawn, -most), most).astype(kind)


def setup_inputs(seed: int = 0) -> dict:
    streams_of = jax.random.split(jax.random.key(seed), 20)
    return {
        "x_in": bell_draw(streams_of[0], (TOKENS, D), 1.0, 6.0, ((0, 8),)),
        "attn_in": bell_draw(streams_of[1], (TOKENS, D), 1.0, 6.0, ((0, 8), (1, 4))),
        "grad_qkv": bell_draw(streams_of[2], (TOKENS, 3 * D), (0.2 * TOKENS ** 0.5), 80.0, ((0, 8), (1, 4))),
        "grad_out": bell_draw(streams_of[3], (TOKENS, D), (0.2 * TOKENS ** 0.5), 80.0, ((0, 8),)),
        "owner": draw_owner(jax.random.fold_in(streams_of[19], 71), 0),
        "step": jax.random.randint(streams_of[5], (1,), 1, 30).astype(jnp.int32),
        "master": bell_draw(streams_of[6], (N_GRP, N_DP * SLOTS, BLK, BLK), 0.02, 0.125, ((0, 4), (1, 8)), jnp.float32),
        "moment": bell_draw(streams_of[7], (N_GRP, N_DP * SLOTS, BLK, BLK), 0.05, 0.3125, ((0, 4), (1, 8)), jnp.float32),
        "second": jnp.clip(jnp.exp(math.log(0.1) - 3.506558 * jax.random.uniform(streams_of[8], (N_GRP, N_DP * SLOTS, BLK, BLK), jnp.float32) ** shard_levels(streams_of[8], (N_GRP, N_DP * SLOTS, BLK, BLK), ((0, 4), (1, 8)), -0.2, 0.2)), 0.003, 0.1),
        "stat_left": draw_stat_left(jax.random.fold_in(streams_of[19], 71), 0),
        "stat_right": draw_stat_right(jax.random.fold_in(streams_of[19], 71), 0),
        "root_left": draw_root_left(jax.random.fold_in(streams_of[19], 71), 0),
        "root_right": draw_root_right(jax.random.fold_in(streams_of[19], 71), 0),
        "qkv_bias": bell_draw(streams_of[13], (3 * D,), 0.5, 3.0, ((0, 4),), jnp.float32),
        "qkv_bias_m": bell_draw(streams_of[14], (3 * D,), 0.2, 1.25, ((0, 4),), jnp.float32),
        "qkv_bias_v": jnp.clip(jnp.exp(math.log(0.3) - 3.4011974 * jax.random.uniform(streams_of[15], (3 * D,), jnp.float32) ** shard_levels(streams_of[15], (3 * D,), ((0, 4),), -0.2, 0.2)), 0.01, 0.3),
        "proj_bias": bell_draw(streams_of[16], (D,), 0.5, 3.0, (), jnp.float32),
        "proj_bias_m": bell_draw(streams_of[17], (D,), 0.2, 1.25, (), jnp.float32),
        "proj_bias_v": jnp.clip(jnp.exp(jax.random.uniform(streams_of[18], (D,), jnp.float32, math.log(0.01), math.log(0.3))), 0.01, 0.3),
    }


beta_one = 0.9
beta_two = 0.95
beta_stat = 0.9
learn_rate = 0.02
weight_decay = 0.1
epsilon = 1e-08
graft_floor = 1e-06

def positions(owner):
    blocks = jnp.arange(NBLK, dtype=jnp.int32)
    same_owner = owner[None, :] == owner[:, None]
    earlier = blocks[None, :] < blocks[:, None]
    slot_rank = lax.optimization_barrier(jnp.sum(jnp.where(same_owner & earlier, 1, 0).astype(jnp.int32), axis=1))
    return (owner * SLOTS + slot_rank).astype(jnp.int32)

def to_blocks(qkv_part, proj_part):
    rows_q = D // BLK
    cols_q = qkv_part.shape[1] // BLK
    first = qkv_part.reshape(rows_q, BLK, cols_q, BLK).transpose(0, 2, 1, 3).reshape(rows_q * cols_q, BLK, BLK)
    rows_p = proj_part.shape[0] // BLK
    second_part = proj_part.reshape(rows_p, BLK, rows_q, BLK).transpose(0, 2, 1, 3).reshape(rows_p * rows_q, BLK, BLK)
    return jnp.concatenate([first, second_part], axis=0)

def from_blocks(blocks):
    rows_q = D // BLK
    cols_q = 3 * D // (N_GRP * BLK)
    rows_p = D // (N_GRP * BLK)
    first = blocks[:NQ].reshape(rows_q, cols_q, BLK, BLK).transpose(0, 2, 1, 3).reshape(D, cols_q * BLK)
    second_part = blocks[NQ:].reshape(rows_p, rows_q, BLK, BLK).transpose(0, 2, 1, 3).reshape(rows_p * BLK, D)
    return (first, second_part)

def adamw(param, first_m, second_m, grad, fix_one, fix_two):
    new_m = beta_one * first_m + (1.0 - beta_one) * grad
    new_v = beta_two * second_m + (1.0 - beta_two) * grad * grad
    new_p = param - learn_rate * (new_m / fix_one) / (jnp.sqrt(new_v / fix_two) + epsilon)
    return (new_p, new_m, new_v)

def reference(x_in, attn_in, grad_qkv, grad_out, owner, step, master, moment, second, stat_left, stat_right, root_left, root_right, qkv_bias, qkv_bias_m, qkv_bias_v, proj_bias, proj_bias_m, proj_bias_v):
    exact = lax.Precision.HIGHEST
    count_f = step[0].astype(jnp.float32)
    fix_one = 1.0 - jnp.power(jnp.float32(beta_one), count_f)
    fix_two = 1.0 - jnp.power(jnp.float32(beta_two), count_f)
    grad_q = jnp.dot(x_in.T, grad_qkv, preferred_element_type=jnp.float32) / TOKENS
    grad_p = jnp.dot(attn_in.T, grad_out, preferred_element_type=jnp.float32) / TOKENS
    width_q = 3 * D // N_GRP
    width_p = D // N_GRP
    grads = jnp.stack([to_blocks(grad_q[:, group * width_q:(group + 1) * width_q], grad_p[group * width_p:(group + 1) * width_p, :]) for group in range(N_GRP)])
    position = positions(owner)
    is_qkv = jnp.arange(NBLK) < NQ
    old_w = master[:, position]
    old_m = moment[:, position]
    old_v = second[:, position]
    old_l = stat_left[:, position]
    old_r = stat_right[:, position]
    left_root = root_left[:, position]
    right_root = root_right[:, position]
    new_v = beta_two * old_v + (1.0 - beta_two) * grads * grads
    adam_dir = grads / (jnp.sqrt(new_v / fix_two) + epsilon)
    half = jnp.einsum('gbij,gbjk->gbik', left_root, grads, precision=exact)
    shampoo_dir = jnp.einsum('gbij,gbjk->gbik', half, right_root, precision=exact)
    adam_sq = lax.optimization_barrier(jnp.sum(adam_dir * adam_dir, axis=(2, 3)))
    shampoo_sq = lax.optimization_barrier(jnp.sum(shampoo_dir * shampoo_dir, axis=(2, 3)))
    adam_tot = jnp.stack([jnp.sum(jnp.where(is_qkv[None, :], adam_sq, 0.0)), jnp.sum(jnp.where(is_qkv[None, :], 0.0, adam_sq))])
    shampoo_tot = jnp.stack([jnp.sum(jnp.where(is_qkv[None, :], shampoo_sq, 0.0)), jnp.sum(jnp.where(is_qkv[None, :], 0.0, shampoo_sq))])
    graft = jnp.sqrt(adam_tot / (shampoo_tot + graft_floor))
    block_graft = jnp.where(is_qkv, graft[0], graft[1])
    new_m = beta_one * old_m + (1.0 - beta_one) * (block_graft[None, :, None, None] * shampoo_dir)
    new_w = old_w - learn_rate * (new_m + weight_decay * old_w)
    new_l = beta_stat * old_l + (1.0 - beta_stat) * jnp.einsum('gbik,gbjk->gbij', grads, grads, precision=exact)
    new_r = beta_stat * old_r + (1.0 - beta_stat) * jnp.einsum('gbki,gbkj->gbij', grads, grads, precision=exact)
    master_new = master.at[:, position].set(new_w)
    moment_new = moment.at[:, position].set(new_m)
    second_new = second.at[:, position].set(new_v)
    left_new = stat_left.at[:, position].set(new_l)
    right_new = stat_right.at[:, position].set(new_r)
    light = new_w.astype(jnp.bfloat16)
    qkv_parts = []
    proj_parts = []
    for group in range(N_GRP):
        first, second_part = from_blocks(light[group])
        qkv_parts.append(first)
        proj_parts.append(second_part)
    qkv_weight = jnp.concatenate(qkv_parts, axis=1)
    proj_weight = jnp.concatenate(proj_parts, axis=0)
    grad_qb = lax.optimization_barrier(jnp.sum(grad_qkv.astype(jnp.float32), axis=0)) / TOKENS
    grad_pb = lax.optimization_barrier(jnp.sum(grad_out.astype(jnp.float32), axis=0)) / TOKENS
    qb_new, qm_new, qv_new = adamw(qkv_bias, qkv_bias_m, qkv_bias_v, grad_qb, fix_one, fix_two)
    pb_new, pm_new, pv_new = adamw(proj_bias, proj_bias_m, proj_bias_v, grad_pb, fix_one, fix_two)
    return (master_new, moment_new, second_new, left_new, right_new, qkv_weight, proj_weight, qb_new, qm_new, qv_new, pb_new, pm_new, pv_new)
```

```python
import jax
import jax.numpy as jnp
from jax import lax
from jax.experimental import pallas as pl
from jax.experimental.pallas import tpu as pltpu
from jax.sharding import PartitionSpec as P

D = 1600


beta_one = 0.9
beta_two = 0.95
beta_stat = 0.9
learn_rate = 0.02
weight_decay = 0.1
epsilon = 1e-08
graft_floor = 1e-06


def positions(owner, slot_count):
    total_blocks = owner.shape[0]
    blocks = jnp.arange(total_blocks, dtype=jnp.int32)
    same_owner = owner[None, :] == owner[:, None]
    earlier = blocks[None, :] < blocks[:, None]
    slot_rank = jnp.sum(jnp.where(same_owner & earlier, 1, 0).astype(jnp.int32), axis=1)
    return owner * slot_count + slot_rank


def adamw(param, first_m, second_m, grad, fix_one, fix_two):
    new_m = beta_one * first_m + (1.0 - beta_one) * grad
    new_v = beta_two * second_m + (1.0 - beta_two) * grad * grad
    new_p = param - learn_rate * (new_m / fix_one) / (jnp.sqrt(new_v / fix_two) + epsilon)
    return (new_p, new_m, new_v)


def place_kernel(split, cols_q, rows_q, pos_ref, left_ref, right_ref, tile_ref, peak_ref):
    b = pl.program_id(0)
    first = b < split
    later = jnp.maximum(b - split, 0)
    i = jnp.where(first, b // cols_q, rows_q + later // rows_q)
    j = jnp.where(first, b % cols_q, cols_q + later % rows_q)
    tile = lax.dot_general(
        left_ref[i], right_ref[j], (((1,), (1,)), ((), ())), preferred_element_type=jnp.float32
    )
    tile_ref[0] = tile
    peak_ref[0] = jnp.full((8, 128), jnp.max(jnp.abs(tile)), jnp.float32)


def place_tiles(left, right, position, split, cols_q, rows_q, spots):
    total = position.shape[0]
    side, depth = left.shape[1:]
    return pl.pallas_call(
        lambda *refs: place_kernel(split, cols_q, rows_q, *refs),
        out_shape=(
            jax.ShapeDtypeStruct((spots, side, side), jnp.float32),
            jax.ShapeDtypeStruct((total, 8, 128), jnp.float32),
        ),
        grid_spec=pltpu.PrefetchScalarGridSpec(
            num_scalar_prefetch=1,
            grid=(total,),
            in_specs=[
                pl.BlockSpec(left.shape, lambda b, pos: (0, 0, 0)),
                pl.BlockSpec(right.shape, lambda b, pos: (0, 0, 0)),
            ],
            out_specs=[
                pl.BlockSpec((1, side, side), lambda b, pos: (pos[b], 0, 0)),
                pl.BlockSpec((1, 8, 128), lambda b, pos: (b, 0, 0)),
            ],
        ),
        compiler_params=pltpu.CompilerParams(vmem_limit_bytes=32 * 1024 * 1024),
    )(position, left, right)


def join_kernel(count, pos_ref, *refs):
    out_ref = refs[count]
    parts = [refs[k][0].astype(jnp.float32) for k in range(count)]
    out_ref[...] = jnp.concatenate(parts, axis=1).astype(out_ref.dtype)


def join_tiles(tiles, position, base, rows, cols):
    side = tiles.shape[1]

    def spot(k):
        return lambda r, pos: (pos[base + r * cols + k], 0, 0)

    return pl.pallas_call(
        lambda *refs: join_kernel(cols, *refs),
        out_shape=jax.ShapeDtypeStruct((rows * side, cols * side), tiles.dtype),
        grid_spec=pltpu.PrefetchScalarGridSpec(
            num_scalar_prefetch=1,
            grid=(rows,),
            in_specs=[pl.BlockSpec((1, side, side), spot(k)) for k in range(cols)],
            out_specs=pl.BlockSpec((side, cols * side), lambda r, pos: (r, 0)),
        ),
        compiler_params=pltpu.CompilerParams(vmem_limit_bytes=32 * 1024 * 1024),
    )(position, *([tiles] * cols))


def sum_kernel(axes, sizes, in_ref, out_ref, *scratch):
    buffers = scratch[: len(axes)]
    send_sems = scratch[len(axes) : 2 * len(axes)]
    recv_sems = scratch[2 * len(axes) :]
    barrier = pltpu.get_barrier_semaphore()
    for axis, size in zip(axes, sizes):
        me = lax.axis_index(axis)
        for k in range(1, size):
            pl.semaphore_signal(
                barrier,
                inc=1,
                device_id={axis: lax.rem(me + k, size)},
                device_id_type=pl.DeviceIdType.MESH,
            )
    pl.semaphore_wait(barrier, sum(size - 1 for size in sizes))
    value = in_ref[...]
    for n, (axis, size) in enumerate(zip(axes, sizes)):
        me = lax.axis_index(axis)
        buffers[n][me] = value
        copies = []
        for k in range(1, size):
            copy = pltpu.make_async_remote_copy(
                src_ref=buffers[n].at[me],
                dst_ref=buffers[n].at[me],
                send_sem=send_sems[n].at[k - 1],
                recv_sem=recv_sems[n].at[k - 1],
                device_id={axis: lax.rem(me + k, size)},
                device_id_type=pl.DeviceIdType.MESH,
            )
            copy.start()
            copies.append(copy)
        for copy in copies:
            copy.wait()
        value = buffers[n][0]
        for k in range(1, size):
            value = value + buffers[n][k]
    out_ref[...] = value


def sum_over(value, axes, collective_id):
    sizes = [lax.axis_size(axis) for axis in axes]
    scratch = [pltpu.VMEM((size,) + value.shape, jnp.float32) for size in sizes]
    scratch += [pltpu.SemaphoreType.DMA((size - 1,)) for size in sizes]
    scratch += [pltpu.SemaphoreType.DMA((size - 1,)) for size in sizes]
    return pl.pallas_call(
        lambda *refs: sum_kernel(axes, sizes, *refs),
        out_shape=jax.ShapeDtypeStruct(value.shape, jnp.float32),
        in_specs=[pl.BlockSpec(memory_space=pltpu.VMEM)],
        out_specs=pl.BlockSpec(memory_space=pltpu.VMEM),
        scratch_shapes=scratch,
        compiler_params=pltpu.CompilerParams(collective_id=collective_id, has_side_effects=True),
    )(value)


def on_device(
    x_in,
    attn_in,
    grad_qkv,
    grad_out,
    owner,
    step,
    master,
    moment,
    second,
    stat_left,
    stat_right,
    root_left,
    root_right,
    qkv_bias,
    qkv_bias_m,
    qkv_bias_v,
    proj_bias,
    proj_bias_m,
    proj_bias_v,
):
    exact = lax.Precision.HIGHEST
    groups = lax.axis_size("dp")
    own_index = lax.axis_index("dp")
    total_blocks = owner.shape[0]
    slot_count = master.shape[1]
    block_size = master.shape[2]
    tokens = x_in.shape[0] * groups
    rows_q = D // block_size
    cols_q = grad_qkv.shape[1] // block_size
    rows_p = attn_in.shape[1] // block_size
    first_kind = rows_q * cols_q
    count_f = step[0].astype(jnp.float32)
    fix_one = 1.0 - jnp.power(jnp.float32(beta_one), count_f)
    fix_two = 1.0 - jnp.power(jnp.float32(beta_two), count_f)
    blocks = jnp.arange(total_blocks, dtype=jnp.int32)
    position = positions(owner, slot_count)
    spots = groups * slot_count
    matches = position[None, :] == jnp.arange(spots, dtype=jnp.int32)[:, None]
    filled = jnp.any(matches, axis=1)
    holder = jnp.sum(jnp.where(matches, blocks[None, :], 0), axis=1)
    my_blocks = lax.dynamic_slice_in_dim(holder, own_index * slot_count, slot_count)
    my_filled = lax.dynamic_slice_in_dim(filled, own_index * slot_count, slot_count)
    filled_f = my_filled.astype(jnp.float32)
    keep = my_filled[:, None, None]

    depth = x_in.shape[0]
    left = jnp.concatenate(
        [
            x_in.T.reshape(rows_q, block_size, depth),
            attn_in.T.reshape(rows_p, block_size, depth),
        ]
    )
    right = jnp.concatenate(
        [
            grad_qkv.T.reshape(cols_q, block_size, depth),
            grad_out.T.reshape(rows_q, block_size, depth),
        ]
    )
    local_tiles, peaks = place_tiles(
        left, right, position, first_kind, cols_q, rows_q, spots
    )

    width_q, width_p = grad_qkv.shape[1], grad_out.shape[1]
    small = jnp.concatenate(
        [
            jnp.sum(grad_qkv, axis=0, dtype=jnp.float32),
            jnp.sum(grad_out, axis=0, dtype=jnp.float32),
            peaks[:, 0, 0],
        ]
    )
    used = small.shape[0]
    padded = -(-used // 1024) * 1024
    small = jnp.pad(small, (0, padded - used)).reshape(8, padded // 8)
    small = sum_over(small, ("dp",), 0).reshape(padded)
    qkv_total = small[:width_q]
    proj_total = small[width_q : width_q + width_p]
    bound = small[width_q + width_p : used]
    spot_bound = jnp.sum(jnp.where(matches, bound[None, :], 0.0), axis=1)
    spot_bound = jnp.where(spot_bound > 0.0, spot_bound, 1.0).reshape(groups, slot_count, 1, 1)
    shrink = 16384.0 / spot_bound
    grow = spot_bound / 16384.0

    pair = own_index // 2
    side = own_index % 2
    pairs = groups // 2
    tiles = local_tiles.reshape(groups, slot_count, block_size, block_size)

    def chunk(array, where):
        return lax.dynamic_index_in_dim(array, where, 0, keepdims=False)

    across = [(d, d ^ 1) for d in range(groups)]
    mine = None
    arrivals = []
    for step_off in list(range(1, pairs)) + [0]:
        target = lax.rem(pair + step_off, pairs)
        theirs = target * 2 + 1 - side
        ours = target * 2 + side
        sent = (chunk(tiles, theirs) * chunk(shrink, theirs)).astype(jnp.float16)
        got = lax.ppermute(sent, "dp", across)
        both = chunk(tiles, ours) * chunk(shrink, ours) + got.astype(jnp.float32)
        if step_off == 0:
            mine = both
        else:
            hop = [(d, ((d // 2 + step_off) % pairs) * 2 + d % 2) for d in range(groups)]
            arrivals.append(lax.ppermute(both.astype(jnp.float16), "dp", hop))
    for arrived in arrivals:
        mine = mine + arrived.astype(jnp.float32)
    grads = jnp.where(keep, mine * (chunk(grow, own_index) / tokens), 0.0)
    old_w = master[0]
    old_m = moment[0]
    old_v = second[0]
    old_l = stat_left[0]
    old_r = stat_right[0]
    new_v = beta_two * old_v + (1.0 - beta_two) * grads * grads
    adam_dir = grads / (jnp.sqrt(new_v / fix_two) + epsilon)
    half = jnp.einsum("sij,sjk->sik", root_left[0], grads, precision=exact)
    shampoo_dir = jnp.einsum("sij,sjk->sik", half, root_right[0], precision=exact)
    is_qkv = my_blocks < first_kind
    adam_sq = jnp.sum(adam_dir * adam_dir, axis=(1, 2)) * filled_f
    shampoo_sq = jnp.sum(shampoo_dir * shampoo_dir, axis=(1, 2)) * filled_f
    sums = [
        jnp.sum(jnp.where(is_qkv, adam_sq, 0.0)),
        jnp.sum(jnp.where(is_qkv, 0.0, adam_sq)),
        jnp.sum(jnp.where(is_qkv, shampoo_sq, 0.0)),
        jnp.sum(jnp.where(is_qkv, 0.0, shampoo_sq)),
    ]
    lane = lax.broadcasted_iota(jnp.int32, (8, 128), 1)
    part = jnp.zeros((8, 128), jnp.float32)
    for n, value in enumerate(sums):
        part = jnp.where(lane == n, value, part)
    total = sum_over(part, ("grp", "dp"), 1)
    graft = jnp.sqrt(total[0, 0:2] / (total[0, 2:4] + graft_floor))
    block_graft = jnp.where(is_qkv, graft[0], graft[1])
    new_m = beta_one * old_m + (1.0 - beta_one) * (block_graft[:, None, None] * shampoo_dir)
    new_w = old_w - learn_rate * (new_m + weight_decay * old_w)
    new_l = beta_stat * old_l + (1.0 - beta_stat) * jnp.einsum(
        "sik,sjk->sij", grads, grads, precision=exact
    )
    new_r = beta_stat * old_r + (1.0 - beta_stat) * jnp.einsum(
        "ski,skj->sij", grads, grads, precision=exact
    )
    master_new = jnp.where(keep, new_w, old_w)
    moment_new = jnp.where(keep, new_m, old_m)
    second_new = jnp.where(keep, new_v, old_v)
    left_new = jnp.where(keep, new_l, old_l)
    right_new = jnp.where(keep, new_r, old_r)
    new_weights = master_new.astype(jnp.bfloat16)
    spread = [new_weights]
    for step_off in range(1, pairs):
        hop = [(d, ((d // 2 + step_off) % pairs) * 2 + d % 2) for d in range(groups)]
        spread.append(lax.ppermute(new_weights, "dp", hop))
    other = [lax.ppermute(part_w, "dp", across) for part_w in spread]
    everyone = jnp.concatenate(spread + other)
    place_owner = owner // 2
    turn = lax.rem(pair - place_owner + pairs, pairs)
    order = jnp.where(owner % 2 == side, turn, pairs + turn)
    where_held = order * slot_count + (position - owner * slot_count)
    qkv_weight = join_tiles(everyone, where_held, 0, rows_q, cols_q)
    proj_weight = join_tiles(everyone, where_held, first_kind, rows_p, rows_q)
    qb_new, qm_new, qv_new = adamw(
        qkv_bias, qkv_bias_m, qkv_bias_v, qkv_total / tokens, fix_one, fix_two
    )
    pb_new, pm_new, pv_new = adamw(
        proj_bias, proj_bias_m, proj_bias_v, proj_total / tokens, fix_one, fix_two
    )
    return (
        master_new[None],
        moment_new[None],
        second_new[None],
        left_new[None],
        right_new[None],
        qkv_weight,
        proj_weight,
        qb_new,
        qm_new,
        qv_new,
        pb_new,
        pm_new,
        pv_new,
    )


def solution(mesh):
    return jax.shard_map(
        on_device,
        mesh=mesh,
        in_specs=(
            P("dp", None),
            P("dp", "grp"),
            P("dp", "grp"),
            P("dp", None),
            P(),
            P(),
            P("grp", "dp", None, None),
            P("grp", "dp", None, None),
            P("grp", "dp", None, None),
            P("grp", "dp", None, None),
            P("grp", "dp", None, None),
            P("grp", "dp", None, None),
            P("grp", "dp", None, None),
            P("grp"),
            P("grp"),
            P("grp"),
            P(),
            P(),
            P(),
        ),
        out_specs=(
            P("grp", "dp", None, None),
            P("grp", "dp", None, None),
            P("grp", "dp", None, None),
            P("grp", "dp", None, None),
            P("grp", "dp", None, None),
            P(None, "grp"),
            P("grp", None),
            P("grp"),
            P("grp"),
            P("grp"),
            P(),
            P(),
            P(),
        ),
        check_vma=False,
    )
```

```python
import jax
import jax.numpy as jnp
from jax import lax
from jax.experimental import pallas as pl
from jax.experimental.pallas import tpu as pltpu
from jax.sharding import PartitionSpec as P

D = 1600


beta_one = 0.9
beta_two = 0.95
beta_stat = 0.9
learn_rate = 0.02
weight_decay = 0.1
epsilon = 1e-08
graft_floor = 1e-06


def positions(owner, slot_count):
    total_blocks = owner.shape[0]
    blocks = jnp.arange(total_blocks, dtype=jnp.int32)
    same_owner = owner[None, :] == owner[:, None]
    earlier = blocks[None, :] < blocks[:, None]
    slot_rank = jnp.sum(jnp.where(same_owner & earlier, 1, 0).astype(jnp.int32), axis=1)
    return owner * slot_count + slot_rank


def adamw(param, first_m, second_m, grad, fix_one, fix_two):
    new_m = beta_one * first_m + (1.0 - beta_one) * grad
    new_v = beta_two * second_m + (1.0 - beta_two) * grad * grad
    new_p = param - learn_rate * (new_m / fix_one) / (jnp.sqrt(new_v / fix_two) + epsilon)
    return (new_p, new_m, new_v)


def place_kernel(split, cols_q, rows_q, pos_ref, left_ref, right_ref, tile_ref, peak_ref):
    b = pl.program_id(0)
    first = b < split
    later = jnp.maximum(b - split, 0)
    i = jnp.where(first, b // cols_q, rows_q + later // rows_q)
    j = jnp.where(first, b % cols_q, cols_q + later % rows_q)
    tile = lax.dot_general(
        left_ref[i], right_ref[j], (((1,), (1,)), ((), ())), preferred_element_type=jnp.float32
    )
    tile_ref[0] = tile
    peak_ref[0] = jnp.full((8, 128), jnp.max(jnp.abs(tile)), jnp.float32)


def place_tiles(left, right, position, split, cols_q, rows_q, spots):
    total = position.shape[0]
    side, depth = left.shape[1:]
    return pl.pallas_call(
        lambda *refs: place_kernel(split, cols_q, rows_q, *refs),
        out_shape=(
            jax.ShapeDtypeStruct((spots, side, side), jnp.float32),
            jax.ShapeDtypeStruct((total, 8, 128), jnp.float32),
        ),
        grid_spec=pltpu.PrefetchScalarGridSpec(
            num_scalar_prefetch=1,
            grid=(total,),
            in_specs=[
                pl.BlockSpec(left.shape, lambda b, pos: (0, 0, 0)),
                pl.BlockSpec(right.shape, lambda b, pos: (0, 0, 0)),
            ],
            out_specs=[
                pl.BlockSpec((1, side, side), lambda b, pos: (pos[b], 0, 0)),
                pl.BlockSpec((1, 8, 128), lambda b, pos: (b, 0, 0)),
            ],
        ),
        compiler_params=pltpu.CompilerParams(vmem_limit_bytes=32 * 1024 * 1024),
    )(position, left, right)


def join_kernel(count, pos_ref, *refs):
    out_ref = refs[count]
    parts = [refs[k][0].astype(jnp.float32) for k in range(count)]
    out_ref[...] = jnp.concatenate(parts, axis=1).astype(out_ref.dtype)


def join_tiles(tiles, position, base, rows, cols):
    side = tiles.shape[1]

    def spot(k):
        return lambda r, pos: (pos[base + r * cols + k], 0, 0)

    return pl.pallas_call(
        lambda *refs: join_kernel(cols, *refs),
        out_shape=jax.ShapeDtypeStruct((rows * side, cols * side), tiles.dtype),
        grid_spec=pltpu.PrefetchScalarGridSpec(
            num_scalar_prefetch=1,
            grid=(rows,),
            in_specs=[pl.BlockSpec((1, side, side), spot(k)) for k in range(cols)],
            out_specs=pl.BlockSpec((side, cols * side), lambda r, pos: (r, 0)),
        ),
        compiler_params=pltpu.CompilerParams(vmem_limit_bytes=32 * 1024 * 1024),
    )(position, *([tiles] * cols))


def sum_kernel(axes, sizes, in_ref, out_ref, *scratch):
    buffers = scratch[: len(axes)]
    send_sems = scratch[len(axes) : 2 * len(axes)]
    recv_sems = scratch[2 * len(axes) :]
    barrier = pltpu.get_barrier_semaphore()
    for axis, size in zip(axes, sizes):
        me = lax.axis_index(axis)
        for k in range(1, size):
            pl.semaphore_signal(
                barrier,
                inc=1,
                device_id={axis: lax.rem(me + k, size)},
                device_id_type=pl.DeviceIdType.MESH,
            )
    pl.semaphore_wait(barrier, sum(size - 1 for size in sizes))
    value = in_ref[...]
    for n, (axis, size) in enumerate(zip(axes, sizes)):
        me = lax.axis_index(axis)
        buffers[n][me] = value
        copies = []
        for k in range(1, size):
            copy = pltpu.make_async_remote_copy(
                src_ref=buffers[n].at[me],
                dst_ref=buffers[n].at[me],
                send_sem=send_sems[n].at[k - 1],
                recv_sem=recv_sems[n].at[k - 1],
                device_id={axis: lax.rem(me + k, size)},
                device_id_type=pl.DeviceIdType.MESH,
            )
            copy.start()
            copies.append(copy)
        for copy in copies:
            copy.wait()
        value = buffers[n][0]
        for k in range(1, size):
            value = value + buffers[n][k]
    out_ref[...] = value


def sum_over(value, axes, collective_id):
    sizes = [lax.axis_size(axis) for axis in axes]
    scratch = [pltpu.VMEM((size,) + value.shape, jnp.float32) for size in sizes]
    scratch += [pltpu.SemaphoreType.DMA((size - 1,)) for size in sizes]
    scratch += [pltpu.SemaphoreType.DMA((size - 1,)) for size in sizes]
    return pl.pallas_call(
        lambda *refs: sum_kernel(axes, sizes, *refs),
        out_shape=jax.ShapeDtypeStruct(value.shape, jnp.float32),
        in_specs=[pl.BlockSpec(memory_space=pltpu.VMEM)],
        out_specs=pl.BlockSpec(memory_space=pltpu.VMEM),
        scratch_shapes=scratch,
        compiler_params=pltpu.CompilerParams(collective_id=collective_id, has_side_effects=True),
    )(value)


def on_device(
    x_in,
    attn_in,
    grad_qkv,
    grad_out,
    owner,
    step,
    master,
    moment,
    second,
    stat_left,
    stat_right,
    root_left,
    root_right,
    qkv_bias,
    qkv_bias_m,
    qkv_bias_v,
    proj_bias,
    proj_bias_m,
    proj_bias_v,
):
    exact = lax.Precision.HIGHEST
    groups = lax.axis_size("dp")
    own_index = lax.axis_index("dp")
    total_blocks = owner.shape[0]
    slot_count = master.shape[1]
    block_size = master.shape[2]
    tokens = x_in.shape[0] * groups
    rows_q = D // block_size
    cols_q = grad_qkv.shape[1] // block_size
    rows_p = attn_in.shape[1] // block_size
    first_kind = rows_q * cols_q
    count_f = step[0].astype(jnp.float32)
    fix_one = 1.0 - jnp.power(jnp.float32(beta_one), count_f)
    fix_two = 1.0 - jnp.power(jnp.float32(beta_two), count_f)
    blocks = jnp.arange(total_blocks, dtype=jnp.int32)
    position = positions(owner, slot_count)
    spots = groups * slot_count
    matches = position[None, :] == jnp.arange(spots, dtype=jnp.int32)[:, None]
    filled = jnp.any(matches, axis=1)
    holder = jnp.sum(jnp.where(matches, blocks[None, :], 0), axis=1)
    my_blocks = lax.dynamic_slice_in_dim(holder, own_index * slot_count, slot_count)
    my_filled = lax.dynamic_slice_in_dim(filled, own_index * slot_count, slot_count)
    filled_f = my_filled.astype(jnp.float32)
    keep = my_filled[:, None, None]

    depth = x_in.shape[0]
    left = jnp.concatenate(
        [
            x_in.T.reshape(rows_q, block_size, depth),
            attn_in.T.reshape(rows_p, block_size, depth),
        ]
    )
    right = jnp.concatenate(
        [
            grad_qkv.T.reshape(cols_q, block_size, depth),
            grad_out.T.reshape(rows_q, block_size, depth),
        ]
    )
    local_tiles, peaks = place_tiles(
        left, right, position, first_kind, cols_q, rows_q, spots
    )

    width_q, width_p = grad_qkv.shape[1], grad_out.shape[1]
    small = jnp.concatenate(
        [
            jnp.sum(grad_qkv, axis=0, dtype=jnp.float32),
            jnp.sum(grad_out, axis=0, dtype=jnp.float32),
            peaks[:, 0, 0],
        ]
    )
    used = small.shape[0]
    padded = -(-used // 1024) * 1024
    small = jnp.pad(small, (0, padded - used)).reshape(8, padded // 8)
    small = sum_over(small, ("dp",), 0).reshape(padded)
    qkv_total = small[:width_q]
    proj_total = small[width_q : width_q + width_p]
    bound = small[width_q + width_p : used]
    spot_bound = jnp.sum(jnp.where(matches, bound[None, :], 0.0), axis=1)
    spot_bound = jnp.where(spot_bound > 0.0, spot_bound, 1.0).reshape(groups, slot_count, 1, 1)
    shrink = 16384.0 / spot_bound
    grow = spot_bound / 16384.0

    pair = own_index // 2
    side = own_index % 2
    pairs = groups // 2
    tiles = local_tiles.reshape(groups, slot_count, block_size, block_size)

    def chunk(array, where):
        return lax.dynamic_index_in_dim(array, where, 0, keepdims=False)

    across = [(d, d ^ 1) for d in range(groups)]
    arrivals = []
    order = list(range(1, pairs))
    if pairs == 4:
        order = [1, 3, 2]
    order = order + [0]
    received = []
    for step_off in order:
        theirs = lax.rem(pair + step_off, pairs) * 2 + 1 - side
        sent = (chunk(tiles, theirs) * chunk(shrink, theirs)).astype(jnp.float16)
        received.append(lax.ppermute(sent, "dp", across))
    after = jnp.int32(0)
    for step_off, got in zip(order, received):
        ours = lax.rem(pair + step_off, pairs) * 2 + side + after
        both = chunk(tiles, ours) * chunk(shrink, ours) + got.astype(jnp.float32)
        if step_off == 0:
            mine = both
        else:
            hop = [(d, ((d // 2 + step_off) % pairs) * 2 + d % 2) for d in range(groups)]
            both = both.astype(jnp.float16)
            arrivals.append(lax.ppermute(both, "dp", hop))
            probe = arrivals[-1][0, 0, 0].astype(jnp.float32)
            after = jnp.minimum((probe == probe).astype(jnp.int32), 0)
    for arrived in arrivals:
        mine = mine + arrived.astype(jnp.float32)
    grads = jnp.where(keep, mine * (chunk(grow, own_index) / tokens), 0.0)
    old_w = master[0]
    old_m = moment[0]
    old_v = second[0]
    old_l = stat_left[0]
    old_r = stat_right[0]
    new_v = beta_two * old_v + (1.0 - beta_two) * grads * grads
    adam_dir = grads / (jnp.sqrt(new_v / fix_two) + epsilon)
    half = jnp.einsum("sij,sjk->sik", root_left[0], grads, precision=exact)
    shampoo_dir = jnp.einsum("sij,sjk->sik", half, root_right[0], precision=exact)
    is_qkv = my_blocks < first_kind
    adam_sq = jnp.sum(adam_dir * adam_dir, axis=(1, 2)) * filled_f
    shampoo_sq = jnp.sum(shampoo_dir * shampoo_dir, axis=(1, 2)) * filled_f
    sums = [
        jnp.sum(jnp.where(is_qkv, adam_sq, 0.0)),
        jnp.sum(jnp.where(is_qkv, 0.0, adam_sq)),
        jnp.sum(jnp.where(is_qkv, shampoo_sq, 0.0)),
        jnp.sum(jnp.where(is_qkv, 0.0, shampoo_sq)),
    ]
    lane = lax.broadcasted_iota(jnp.int32, (8, 128), 1)
    part = jnp.zeros((8, 128), jnp.float32)
    for n, value in enumerate(sums):
        part = jnp.where(lane == n, value, part)
    total = sum_over(part, ("grp", "dp"), 1)
    graft = jnp.sqrt(total[0, 0:2] / (total[0, 2:4] + graft_floor))
    block_graft = jnp.where(is_qkv, graft[0], graft[1])
    new_m = beta_one * old_m + (1.0 - beta_one) * (block_graft[:, None, None] * shampoo_dir)
    new_w = old_w - learn_rate * (new_m + weight_decay * old_w)
    new_l = beta_stat * old_l + (1.0 - beta_stat) * jnp.einsum(
        "sik,sjk->sij", grads, grads, precision=exact
    )
    new_r = beta_stat * old_r + (1.0 - beta_stat) * jnp.einsum(
        "ski,skj->sij", grads, grads, precision=exact
    )
    master_new = jnp.where(keep, new_w, old_w)
    moment_new = jnp.where(keep, new_m, old_m)
    second_new = jnp.where(keep, new_v, old_v)
    left_new = jnp.where(keep, new_l, old_l)
    right_new = jnp.where(keep, new_r, old_r)
    new_weights = master_new.astype(jnp.bfloat16)
    spread = [new_weights]
    turns = None
    if pairs == 4:
        up = [(d, d + 2) for d in range(groups - 2)]
        down = [(d + 2, d) for d in range(groups - 2)]
        from_low, from_high = [new_weights], [new_weights]
        for k in range(1, pairs):
            from_low.append(lax.ppermute(from_low[-1], "dp", up))
            from_high.append(lax.ppermute(from_high[-1], "dp", down))
        rows = []
        for z in range(pairs):
            found = [(k, 0) for k in range(1, z + 1)] + [(k, 1) for k in range(1, pairs - z)]
            rows.append(sorted(found))
        turns = [[0] * pairs for _ in range(pairs)]
        other = [lax.ppermute(new_weights, "dp", across)]
        for m in range(pairs - 1):
            value = None
            probe = other[-1][0, 0, 0].astype(jnp.float32)
            here = pair + jnp.minimum((probe == probe).astype(jnp.int32), 0)
            for z in range(pairs):
                k, way = rows[z][m]
                turns[z][z + k if way else z - k] = m + 1
                part_w = (from_low, from_high)[way][k]
                value = part_w if value is None else jnp.where(here == z, part_w, value)
            spread.append(value)
            other.append(lax.ppermute(value, "dp", across))
    else:
        for step_off in range(1, pairs):
            hop = [(d, ((d // 2 + step_off) % pairs) * 2 + d % 2) for d in range(groups)]
            spread.append(lax.ppermute(new_weights, "dp", hop))
        other = [lax.ppermute(part_w, "dp", across) for part_w in spread]
    everyone = jnp.concatenate(spread + other)
    place_owner = owner // 2
    turn = lax.rem(pair - place_owner + pairs, pairs)
    if turns is not None:
        turn = jnp.zeros_like(owner)
        for z in range(pairs):
            for origin in range(pairs):
                hit = (pair == z) & (place_owner == origin)
                turn = jnp.where(hit, turns[z][origin], turn)
    held = jnp.where(owner % 2 == side, turn, pairs + turn)
    where_held = held * slot_count + (position - owner * slot_count)
    qkv_weight = join_tiles(everyone, where_held, 0, rows_q, cols_q)
    proj_weight = join_tiles(everyone, where_held, first_kind, rows_p, rows_q)
    qb_new, qm_new, qv_new = adamw(
        qkv_bias, qkv_bias_m, qkv_bias_v, qkv_total / tokens, fix_one, fix_two
    )
    pb_new, pm_new, pv_new = adamw(
        proj_bias, proj_bias_m, proj_bias_v, proj_total / tokens, fix_one, fix_two
    )
    return (
        master_new[None],
        moment_new[None],
        second_new[None],
        left_new[None],
        right_new[None],
        qkv_weight,
        proj_weight,
        qb_new,
        qm_new,
        qv_new,
        pb_new,
        pm_new,
        pv_new,
    )


def solution(mesh):
    return jax.shard_map(
        on_device,
        mesh=mesh,
        in_specs=(
            P("dp", None),
            P("dp", "grp"),
            P("dp", "grp"),
            P("dp", None),
            P(),
            P(),
            P("grp", "dp", None, None),
            P("grp", "dp", None, None),
            P("grp", "dp", None, None),
            P("grp", "dp", None, None),
            P("grp", "dp", None, None),
            P("grp", "dp", None, None),
            P("grp", "dp", None, None),
            P("grp"),
            P("grp"),
            P("grp"),
            P(),
            P(),
            P(),
        ),
        out_specs=(
            P("grp", "dp", None, None),
            P("grp", "dp", None, None),
            P("grp", "dp", None, None),
            P("grp", "dp", None, None),
            P("grp", "dp", None, None),
            P(None, "grp"),
            P("grp", None),
            P("grp"),
            P("grp"),
            P("grp"),
            P(),
            P(),
            P(),
        ),
        check_vma=False,
    )
```

```python
import jax
import jax.numpy as jnp
from jax import lax
from jax.experimental import pallas as pl
from jax.experimental.pallas import tpu as pltpu
from jax.sharding import PartitionSpec as P

D = 1600


beta_one = 0.9
beta_two = 0.95
beta_stat = 0.9
learn_rate = 0.02
weight_decay = 0.1
epsilon = 1e-08
graft_floor = 1e-06


def positions(owner, slot_count):
    total_blocks = owner.shape[0]
    blocks = jnp.arange(total_blocks, dtype=jnp.int32)
    same_owner = owner[None, :] == owner[:, None]
    earlier = blocks[None, :] < blocks[:, None]
    slot_rank = jnp.sum(jnp.where(same_owner & earlier, 1, 0).astype(jnp.int32), axis=1)
    return owner * slot_count + slot_rank


def adamw(param, first_m, second_m, grad, fix_one, fix_two):
    new_m = beta_one * first_m + (1.0 - beta_one) * grad
    new_v = beta_two * second_m + (1.0 - beta_two) * grad * grad
    new_p = param - learn_rate * (new_m / fix_one) / (jnp.sqrt(new_v / fix_two) + epsilon)
    return (new_p, new_m, new_v)


def place_kernel(
    split, cols_q, rows_q, slots, holder_ref, used_ref, left_ref, right_ref, tile_ref, peak_ref
):
    o = pl.program_id(0)
    peak_ref[...] = jnp.zeros_like(peak_ref)
    side = left_ref.shape[1]
    for s in range(slots):
        b = holder_ref[o * slots + s]

        @pl.when(used_ref[o * slots + s] > 0)
        def _():
            first = b < split
            later = jnp.maximum(b - split, 0)
            i = jnp.where(first, b // cols_q, rows_q + later // rows_q)
            j = jnp.where(first, b % cols_q, cols_q + later % rows_q)
            tile = lax.dot_general(
                left_ref[i],
                right_ref[j],
                (((1,), (1,)), ((), ())),
                preferred_element_type=jnp.float32,
            )
            tile_ref[0, :, s * side : (s + 1) * side] = tile
            peak_ref[0, s : s + 1, :] = jnp.full((1, 128), jnp.max(jnp.abs(tile)), jnp.float32)


def place_tiles(left, right, holder, used, split, cols_q, rows_q, groups, slots):
    side, depth = left.shape[1:]
    return pl.pallas_call(
        lambda *refs: place_kernel(split, cols_q, rows_q, slots, *refs),
        out_shape=(
            jax.ShapeDtypeStruct((groups, side, slots * side), jnp.float32),
            jax.ShapeDtypeStruct((groups, slots, 128), jnp.float32),
        ),
        grid_spec=pltpu.PrefetchScalarGridSpec(
            num_scalar_prefetch=2,
            grid=(groups,),
            in_specs=[
                pl.BlockSpec(left.shape, lambda o, h, u: (0, 0, 0)),
                pl.BlockSpec(right.shape, lambda o, h, u: (0, 0, 0)),
            ],
            out_specs=[
                pl.BlockSpec((1, side, slots * side), lambda o, h, u: (o, 0, 0)),
                pl.BlockSpec((1, slots, 128), lambda o, h, u: (o, 0, 0)),
            ],
        ),
        compiler_params=pltpu.CompilerParams(vmem_limit_bytes=32 * 1024 * 1024),
    )(holder, used, left, right)


def join_kernel(count, pos_ref, *refs):
    out_ref = refs[count]
    parts = [refs[k][0].astype(jnp.float32) for k in range(count)]
    out_ref[...] = jnp.concatenate(parts, axis=1).astype(out_ref.dtype)


def join_tiles(tiles, position, base, rows, cols):
    side = tiles.shape[1]

    def spot(k):
        return lambda r, pos: (pos[base + r * cols + k], 0, 0)

    return pl.pallas_call(
        lambda *refs: join_kernel(cols, *refs),
        out_shape=jax.ShapeDtypeStruct((rows * side, cols * side), tiles.dtype),
        grid_spec=pltpu.PrefetchScalarGridSpec(
            num_scalar_prefetch=1,
            grid=(rows,),
            in_specs=[pl.BlockSpec((1, side, side), spot(k)) for k in range(cols)],
            out_specs=pl.BlockSpec((side, cols * side), lambda r, pos: (r, 0)),
        ),
        compiler_params=pltpu.CompilerParams(vmem_limit_bytes=32 * 1024 * 1024),
    )(position, *([tiles] * cols))


def sum_kernel(axes, sizes, in_ref, out_ref, *scratch):
    buffers = scratch[: len(axes)]
    send_sems = scratch[len(axes) : 2 * len(axes)]
    recv_sems = scratch[2 * len(axes) :]
    barrier = pltpu.get_barrier_semaphore()
    for axis, size in zip(axes, sizes):
        me = lax.axis_index(axis)
        for k in range(1, size):
            pl.semaphore_signal(
                barrier,
                inc=1,
                device_id={axis: lax.rem(me + k, size)},
                device_id_type=pl.DeviceIdType.MESH,
            )
    pl.semaphore_wait(barrier, sum(size - 1 for size in sizes))
    value = in_ref[...]
    for n, (axis, size) in enumerate(zip(axes, sizes)):
        me = lax.axis_index(axis)
        buffers[n][me] = value
        copies = []
        for k in range(1, size):
            copy = pltpu.make_async_remote_copy(
                src_ref=buffers[n].at[me],
                dst_ref=buffers[n].at[me],
                send_sem=send_sems[n].at[k - 1],
                recv_sem=recv_sems[n].at[k - 1],
                device_id={axis: lax.rem(me + k, size)},
                device_id_type=pl.DeviceIdType.MESH,
            )
            copy.start()
            copies.append(copy)
        for copy in copies:
            copy.wait()
        value = buffers[n][0]
        for k in range(1, size):
            value = value + buffers[n][k]
    out_ref[...] = value


def sum_over(value, axes, collective_id):
    sizes = [lax.axis_size(axis) for axis in axes]
    scratch = [pltpu.VMEM((size,) + value.shape, jnp.float32) for size in sizes]
    scratch += [pltpu.SemaphoreType.DMA((size - 1,)) for size in sizes]
    scratch += [pltpu.SemaphoreType.DMA((size - 1,)) for size in sizes]
    return pl.pallas_call(
        lambda *refs: sum_kernel(axes, sizes, *refs),
        out_shape=jax.ShapeDtypeStruct(value.shape, jnp.float32),
        in_specs=[pl.BlockSpec(memory_space=pltpu.VMEM)],
        out_specs=pl.BlockSpec(memory_space=pltpu.VMEM),
        scratch_shapes=scratch,
        compiler_params=pltpu.CompilerParams(collective_id=collective_id, has_side_effects=True),
    )(value)


def on_device(
    x_in,
    attn_in,
    grad_qkv,
    grad_out,
    owner,
    step,
    master,
    moment,
    second,
    stat_left,
    stat_right,
    root_left,
    root_right,
    qkv_bias,
    qkv_bias_m,
    qkv_bias_v,
    proj_bias,
    proj_bias_m,
    proj_bias_v,
):
    exact = lax.Precision.HIGHEST
    groups = lax.axis_size("dp")
    own_index = lax.axis_index("dp")
    total_blocks = owner.shape[0]
    slot_count = master.shape[1]
    block_size = master.shape[2]
    tokens = x_in.shape[0] * groups
    rows_q = D // block_size
    cols_q = grad_qkv.shape[1] // block_size
    rows_p = attn_in.shape[1] // block_size
    first_kind = rows_q * cols_q
    count_f = step[0].astype(jnp.float32)
    fix_one = 1.0 - jnp.power(jnp.float32(beta_one), count_f)
    fix_two = 1.0 - jnp.power(jnp.float32(beta_two), count_f)
    blocks = jnp.arange(total_blocks, dtype=jnp.int32)
    position = positions(owner, slot_count)
    spots = groups * slot_count
    matches = position[None, :] == jnp.arange(spots, dtype=jnp.int32)[:, None]
    filled = jnp.any(matches, axis=1)
    holder = jnp.sum(jnp.where(matches, blocks[None, :], 0), axis=1)
    my_blocks = lax.dynamic_slice_in_dim(holder, own_index * slot_count, slot_count)
    my_filled = lax.dynamic_slice_in_dim(filled, own_index * slot_count, slot_count)
    filled_f = my_filled.astype(jnp.float32)
    keep = my_filled[:, None, None]

    depth = x_in.shape[0]
    left = jnp.concatenate(
        [
            x_in.T.reshape(rows_q, block_size, depth),
            attn_in.T.reshape(rows_p, block_size, depth),
        ]
    )
    right = jnp.concatenate(
        [
            grad_qkv.T.reshape(cols_q, block_size, depth),
            grad_out.T.reshape(rows_q, block_size, depth),
        ]
    )
    local_tiles, peaks = place_tiles(
        left,
        right,
        holder,
        filled.astype(jnp.int32),
        first_kind,
        cols_q,
        rows_q,
        groups,
        slot_count,
    )

    width_q, width_p = grad_qkv.shape[1], grad_out.shape[1]
    small = jnp.concatenate(
        [
            jnp.sum(grad_qkv, axis=0, dtype=jnp.float32),
            jnp.sum(grad_out, axis=0, dtype=jnp.float32),
            peaks[:, :, 0].reshape(spots),
        ]
    )
    used = small.shape[0]
    padded = -(-used // 1024) * 1024
    small = jnp.pad(small, (0, padded - used)).reshape(8, padded // 8)
    small = sum_over(small, ("dp",), 0).reshape(padded)
    qkv_total = small[:width_q]
    proj_total = small[width_q : width_q + width_p]
    bound = small[width_q + width_p : used]
    spot_bound = jnp.where(bound > 0.0, bound, 1.0).reshape(groups, 1, slot_count)
    spot_bound = jnp.repeat(spot_bound, block_size, axis=2)
    shrink = 16384.0 / spot_bound
    grow = spot_bound / 16384.0

    pair = own_index // 2
    side = own_index % 2
    pairs = groups // 2
    tiles = local_tiles

    def chunk(array, where):
        return lax.dynamic_index_in_dim(array, where, 0, keepdims=False)

    across = [(d, d ^ 1) for d in range(groups)]
    arrivals = []
    order = list(range(1, pairs))
    if pairs == 4:
        order = [1, 3, 2]
    order = order + [0]
    received = []
    for step_off in order:
        theirs = lax.rem(pair + step_off, pairs) * 2 + 1 - side
        sent = (chunk(tiles, theirs) * chunk(shrink, theirs)).astype(jnp.float16)
        received.append(lax.ppermute(sent, "dp", across))
    after = jnp.int32(0)
    for step_off, got in zip(order, received):
        ours = lax.rem(pair + step_off, pairs) * 2 + side
        both = chunk(tiles, ours + after) * chunk(shrink, ours) + got.astype(jnp.float32)
        if step_off == 0:
            mine = both
        else:
            hop = [(d, ((d // 2 + step_off) % pairs) * 2 + d % 2) for d in range(groups)]
            both = both.astype(jnp.float16)
            arrivals.append(lax.ppermute(both, "dp", hop))
            probe = arrivals[-1][0, 0].astype(jnp.float32)
            after = jnp.minimum((probe == probe).astype(jnp.int32), 0)
    for arrived in arrivals:
        mine = mine + arrived.astype(jnp.float32)
    mine = mine * (chunk(grow, own_index) / tokens)
    mine = mine.reshape(block_size, slot_count, block_size).transpose(1, 0, 2)
    grads = jnp.where(keep, mine, 0.0)
    old_w = master[0]
    old_m = moment[0]
    old_v = second[0]
    old_l = stat_left[0]
    old_r = stat_right[0]
    new_v = beta_two * old_v + (1.0 - beta_two) * grads * grads
    adam_dir = grads / (jnp.sqrt(new_v / fix_two) + epsilon)
    half = jnp.einsum("sij,sjk->sik", root_left[0], grads, precision=exact)
    shampoo_dir = jnp.einsum("sij,sjk->sik", half, root_right[0], precision=exact)
    is_qkv = my_blocks < first_kind
    adam_sq = jnp.sum(adam_dir * adam_dir, axis=(1, 2)) * filled_f
    shampoo_sq = jnp.sum(shampoo_dir * shampoo_dir, axis=(1, 2)) * filled_f
    sums = [
        jnp.sum(jnp.where(is_qkv, adam_sq, 0.0)),
        jnp.sum(jnp.where(is_qkv, 0.0, adam_sq)),
        jnp.sum(jnp.where(is_qkv, shampoo_sq, 0.0)),
        jnp.sum(jnp.where(is_qkv, 0.0, shampoo_sq)),
    ]
    lane = lax.broadcasted_iota(jnp.int32, (8, 128), 1)
    part = jnp.zeros((8, 128), jnp.float32)
    for n, value in enumerate(sums):
        part = jnp.where(lane == n, value, part)
    total = sum_over(part, ("grp", "dp"), 1)
    graft = jnp.sqrt(total[0, 0:2] / (total[0, 2:4] + graft_floor))
    block_graft = jnp.where(is_qkv, graft[0], graft[1])
    new_m = beta_one * old_m + (1.0 - beta_one) * (block_graft[:, None, None] * shampoo_dir)
    new_w = old_w - learn_rate * (new_m + weight_decay * old_w)
    new_l = beta_stat * old_l + (1.0 - beta_stat) * jnp.einsum(
        "sik,sjk->sij", grads, grads, precision=exact
    )
    new_r = beta_stat * old_r + (1.0 - beta_stat) * jnp.einsum(
        "ski,skj->sij", grads, grads, precision=exact
    )
    master_new = jnp.where(keep, new_w, old_w)
    moment_new = jnp.where(keep, new_m, old_m)
    second_new = jnp.where(keep, new_v, old_v)
    left_new = jnp.where(keep, new_l, old_l)
    right_new = jnp.where(keep, new_r, old_r)
    new_weights = master_new.astype(jnp.bfloat16)
    spread = [new_weights]
    turns = None
    if pairs == 4:
        up = [(d, d + 2) for d in range(groups - 2)]
        down = [(d + 2, d) for d in range(groups - 2)]
        from_low, from_high = [new_weights], [new_weights]
        for k in range(1, pairs):
            from_low.append(lax.ppermute(from_low[-1], "dp", up))
            from_high.append(lax.ppermute(from_high[-1], "dp", down))
        rows = []
        for z in range(pairs):
            found = [(k, 0) for k in range(1, z + 1)] + [(k, 1) for k in range(1, pairs - z)]
            rows.append(sorted(found))
        turns = [[0] * pairs for _ in range(pairs)]
        other = [lax.ppermute(new_weights, "dp", across)]
        for m in range(pairs - 1):
            value = None
            probe = other[-1][0, 0, 0].astype(jnp.float32)
            here = pair + jnp.minimum((probe == probe).astype(jnp.int32), 0)
            for z in range(pairs):
                k, way = rows[z][m]
                turns[z][z + k if way else z - k] = m + 1
                part_w = (from_low, from_high)[way][k]
                value = part_w if value is None else jnp.where(here == z, part_w, value)
            spread.append(value)
            other.append(lax.ppermute(value, "dp", across))
    else:
        for step_off in range(1, pairs):
            hop = [(d, ((d // 2 + step_off) % pairs) * 2 + d % 2) for d in range(groups)]
            spread.append(lax.ppermute(new_weights, "dp", hop))
        other = [lax.ppermute(part_w, "dp", across) for part_w in spread]
    everyone = jnp.concatenate(spread + other)
    place_owner = owner // 2
    turn = lax.rem(pair - place_owner + pairs, pairs)
    if turns is not None:
        turn = jnp.zeros_like(owner)
        for z in range(pairs):
            for origin in range(pairs):
                hit = (pair == z) & (place_owner == origin)
                turn = jnp.where(hit, turns[z][origin], turn)
    held = jnp.where(owner % 2 == side, turn, pairs + turn)
    where_held = held * slot_count + (position - owner * slot_count)
    qkv_weight = join_tiles(everyone, where_held, 0, rows_q, cols_q)
    proj_weight = join_tiles(everyone, where_held, first_kind, rows_p, rows_q)
    qb_new, qm_new, qv_new = adamw(
        qkv_bias, qkv_bias_m, qkv_bias_v, qkv_total / tokens, fix_one, fix_two
    )
    pb_new, pm_new, pv_new = adamw(
        proj_bias, proj_bias_m, proj_bias_v, proj_total / tokens, fix_one, fix_two
    )
    return (
        master_new[None],
        moment_new[None],
        second_new[None],
        left_new[None],
        right_new[None],
        qkv_weight,
        proj_weight,
        qb_new,
        qm_new,
        qv_new,
        pb_new,
        pm_new,
        pv_new,
    )


def solution(mesh):
    return jax.shard_map(
        on_device,
        mesh=mesh,
        in_specs=(
            P("dp", None),
            P("dp", "grp"),
            P("dp", "grp"),
            P("dp", None),
            P(),
            P(),
            P("grp", "dp", None, None),
            P("grp", "dp", None, None),
            P("grp", "dp", None, None),
            P("grp", "dp", None, None),
            P("grp", "dp", None, None),
            P("grp", "dp", None, None),
            P("grp", "dp", None, None),
            P("grp"),
            P("grp"),
            P("grp"),
            P(),
            P(),
            P(),
        ),
        out_specs=(
            P("grp", "dp", None, None),
            P("grp", "dp", None, None),
            P("grp", "dp", None, None),
            P("grp", "dp", None, None),
            P("grp", "dp", None, None),
            P(None, "grp"),
            P("grp", None),
            P("grp"),
            P("grp"),
            P("grp"),
            P(),
            P(),
            P(),
        ),
        check_vma=False,
    )
```
